32 devices in a mesh: seq: 2 (over x), head: 4 (over z), dp: 4 (over y, core).
Axes of the slice: x: 2, y: 2, z: 4, core: 2. Of those that a mesh axis runs over, the one named last changes fastest.
Arguments:
- queries: bfloat16 [4, 512, 64, 128], P('dp', 'seq', 'head'), may hold values from -6 to 6
- keys: bfloat16 [4, 512, 8, 128], P('dp', 'seq', 'head'), may hold values from -6 to 6
- values: bfloat16 [4, 512, 8, 128], P('dp', 'seq', 'head'), may hold values from -6 to 6
- attn_out: bfloat16 [4, 512, 64, 128], P('dp', 'seq', 'head'), may hold values from -6 to 6
- out_grad: bfloat16 [4, 512, 64, 128], P('dp', 'seq', 'head'), may hold values from -6 to 6
- gate_values: float32 [4, 64, 512], P('dp', 'head', 'seq'), may hold values from 0.05 to 0.95
- log_totals: float32 [4, 64, 512], P('dp', 'head', 'seq'), may hold values from 3 to 5
- hidden: bfloat16 [4, 512, 5120], P('dp', 'seq', 'head'), may hold values from -6 to 6
- block_ids: int32 [4, 8, 8, 16], P('dp', 'seq', 'head'), may hold values from 0 to 7, as said below
- block_valid: int32 [4, 8, 8, 16], P('dp', 'seq', 'head'), may hold values from 0 to 1
Outputs:
- query_grad: bfloat16 [4, 512, 64, 128], P('dp', 'seq', 'head')
- key_grad: bfloat16 [4, 512, 8, 128], P('dp', 'seq', 'head')
- value_grad: bfloat16 [4, 512, 8, 128], P('dp', 'seq', 'head')
- gate_weight_grad: float32 [64, 5120], P(None, 'head')
The draws below stay inside these ranges and needn't reach their ends.
Inputs may be any that keep to these rules, and one draw needn't show every extreme that they name: `block_ids`: for query tile t and key head k, the slots whose block_valid is 1 name distinct blocks of index at most t, among them block t itself and block 0; exactly min(16, t + 1) slots are valid. The ids of the other slots are any blocks, and may repeat a valid one.
All inputs are finite; a program needn't handle non-finite values.
Results may differ from the reference program's by a relative error of at most 0.025.
Values may be sent and summed in bfloat16 or wider, within the bound.
No kernel may reach another device: no remote copies, remote signals or barrier semaphores. Data moves between devices by JAX's collectives and lax.ppermute only.
A program may use at most 128 MiB of HBM per device.

```python
import jax
import jax.numpy as jnp
from jax import lax

D = 5120
HQ = 64
KVH = 8
DH = 128
BLK = 64
NSEL = 16
TOK_DEV = 256
GROUP = 8
BATCH = 4
SEQLEN = 512
TILES = 8
N_SEQ = 2


def choose_blocks(key):
    seeded = jax.random.fold_in(key, 17)
    rank_key, order_key = jax.random.split(seeded)
    filler_key = jax.random.fold_in(seeded, 5)
    near_key, far_key, coin_key = jax.random.split(filler_key, 3)
    width_all = TILES + NSEL
    candidate = jnp.arange(width_all, dtype=jnp.int32)[None, None, None, :]
    tile_of = jnp.arange(TILES, dtype=jnp.int32)[None, :, None, None]
    random_part = jax.random.randint(rank_key, (BATCH, TILES, KVH, width_all), 0, 1 << 20)
    ranking = random_part * width_all + candidate
    ranking = jnp.where(candidate <= tile_of, ranking, -1 - candidate)
    ranking = jnp.where(candidate == 0, 1 << 30, ranking)
    ranking = jnp.where(candidate == tile_of, (1 << 30) + 1, ranking)
    best_scores, best_slots = lax.top_k(ranking, NSEL)
    usable = (best_scores >= 0).astype(jnp.int32)
    chosen = (best_slots % TILES).astype(jnp.int32)
    shuffle_keys = jax.random.randint(order_key, (BATCH, TILES, KVH, NSEL), 0, 1 << 20) * NSEL + jnp.arange(NSEL, dtype=jnp.int32)
    shuffle = jnp.argsort(shuffle_keys, axis=-1)
    chosen = jnp.take_along_axis(chosen, shuffle, axis=-1)
    usable = jnp.take_along_axis(usable, shuffle, axis=-1)
    slot_shape = (BATCH, TILES, KVH, NSEL)
    near = jax.random.randint(near_key, slot_shape, 0, 1 << 20) % (tile_of + 1)
    far = jax.random.randint(far_key, slot_shape, 0, TILES)
    coin = jax.random.randint(coin_key, slot_shape, 0, 2)
    filler = jnp.where(coin == 0, near, far).astype(jnp.int32)
    chosen = jnp.where(usable > 0, chosen, filler).astype(jnp.int32)
    return (chosen, usable)


def draw_block_ids(key, part):
    return choose_blocks(key)[0]


def draw_block_valid(key, part):
    return choose_blocks(key)[1]


def block_scale(key, dims, cuts, smallest, largest):
    loudness = 1.0
    for position, blocks in cuts:
        heights = jax.random.uniform(jax.random.fold_in(jax.random.fold_in(key, 6), position), (blocks,), jnp.float32, smallest / len(cuts), largest / len(cuts))
        loudness = loudness * jnp.repeat(jnp.exp(heights), dims[position] // blocks).reshape((-1,) + (1,) * (len(dims) - 1 - position))
    return loudness


def bell_draw(rng, extent, spread, limit, cuts=(), kind=jnp.bfloat16):
    drawn = jax.random.normal(rng, extent, jnp.float32) * spread
    if len(cuts) > 0:
        drawn = block_scale(rng, extent, cuts, -0.22, 0.18) * drawn
    return jnp.clip(drawn, min=-limit, max=limit).astype(kind)


def setup_inputs(seed: int = 0) -> dict:
    splits = jax.random.split(jax.random.key(seed), 11)
    return {
        "queries": bell_draw(splits[0], (BATCH, SEQLEN, HQ, DH), 1.0, 6.0, ((0, 4), (1, 2), (2, 4))),
        "keys": bell_draw(splits[1], (BATCH, SEQLEN, KVH, DH), 1.0, 6.0, ((0, 4), (1, 2), (2, 4))),
        "values": bell_draw(splits[2], (BATCH, SEQLEN, KVH, DH), 1.0, 6.0, ((0, 4), (1, 2), (2, 4))),
        "attn_out": bell_draw(splits[3], (BATCH, SEQLEN, HQ, DH), 1.0, 6.0, ((0, 4), (1, 2), (2, 4))),
        "out_grad": bell_draw(splits[4], (BATCH, SEQLEN, HQ, DH), 1.0, 6.0, ((0, 4), (1, 2), (2, 4))),
        "gate_values": jnp.clip(0.05 + 0.9 * jax.random.uniform(splits[5], (BATCH, HQ, SEQLEN), jnp.float32) ** block_scale(splits[5], (BATCH, HQ, SEQLEN), ((0, 4), (1, 4), (2, 2)), -0.2, 0.2), 0.05, 0.95),
        "log_totals": jnp.clip(3.0 + 2.0 * jax.random.uniform(splits[6], (BATCH, HQ, SEQLEN), jnp.float32) ** block_scale(splits[6], (BATCH, HQ, SEQLEN), ((0, 4), (1, 4), (2, 2)), -0.2, 0.2), 3.0, 5.0),
        "hidden": bell_draw(splits[7], (BATCH, SEQLEN, D), 1.0, 6.0, ((0, 4), (1, 2), (2, 4))),
        "block_ids": draw_block_ids(jax.random.fold_in(splits[10], 71), 0),
        "block_valid": draw_block_valid(jax.random.fold_in(splits[10], 71), 0),
    }


def reference(queries, keys, values, attn_out, out_grad, gate_values, log_totals, hidden, block_ids, block_valid):
    factor = DH ** -0.5
    tiles_dev = TOK_DEV // BLK
    key_blocks = keys.reshape(BATCH, TILES, BLK, KVH, DH)
    value_blocks = values.reshape(BATCH, TILES, BLK, KVH, DH)
    batch_index = jnp.arange(BATCH, dtype=jnp.int32)[:, None, None]
    kv_index = jnp.arange(KVH, dtype=jnp.int32)[None, :, None]
    offsets = jnp.arange(BLK, dtype=jnp.int32)

    def tile_step(partial_value, tile_index):
        first_row = tile_index * BLK
        query_tile = lax.dynamic_slice_in_dim(queries, first_row, BLK, 1).reshape(BATCH, BLK, KVH, GROUP, DH).astype(jnp.float32)
        output_tile = lax.dynamic_slice_in_dim(attn_out, first_row, BLK, 1).reshape(BATCH, BLK, KVH, GROUP, DH).astype(jnp.float32)
        upstream = lax.dynamic_slice_in_dim(out_grad, first_row, BLK, 1).reshape(BATCH, BLK, KVH, GROUP, DH).astype(jnp.float32)
        gate_tile = lax.dynamic_slice_in_dim(gate_values, first_row, BLK, 2).reshape(BATCH, KVH, GROUP, BLK)
        totals = lax.dynamic_slice_in_dim(log_totals, first_row, BLK, 2).reshape(BATCH, KVH, GROUP, BLK)
        chosen = lax.dynamic_index_in_dim(block_ids, tile_index, 1, keepdims=False)
        usable = lax.dynamic_index_in_dim(block_valid, tile_index, 1, keepdims=False) > 0
        key_sel = key_blocks[batch_index, chosen, :, kv_index, :].astype(jnp.float32)
        value_sel = value_blocks[batch_index, chosen, :, kv_index, :].astype(jnp.float32)
        gates_by_row = jnp.transpose(gate_tile, (0, 3, 1, 2))
        grad_low = lax.optimization_barrier((gates_by_row[..., None] * upstream).astype(jnp.bfloat16))
        grad_output = grad_low.astype(jnp.float32)
        row_delta = jnp.transpose(jnp.sum(grad_output * output_tile, axis=-1), (0, 2, 3, 1))
        gate_grad = jnp.sum(upstream * output_tile, axis=-1)
        logit_grad = (gate_grad * gates_by_row * (1.0 - gates_by_row)).astype(jnp.bfloat16)
        scores = jnp.einsum("bikgd,bknjd->bkginj", query_tile, key_sel) * factor
        query_pos = first_row + offsets
        key_pos = chosen[..., None] * BLK + offsets
        allowed = usable[:, :, None, :, None] & (key_pos[:, :, None, :, :] <= query_pos[None, None, :, None, None])
        probability = jnp.where(allowed[:, :, None], jnp.exp(scores - totals[..., None, None]), 0.0)
        prob_grad = jnp.einsum("bikgd,bknjd->bkginj", grad_output, value_sel)
        dscore = lax.optimization_barrier((probability * (prob_grad - row_delta[..., None, None])).astype(jnp.bfloat16)).astype(jnp.float32)
        prob_low = lax.optimization_barrier(probability.astype(jnp.bfloat16)).astype(jnp.float32)
        query_part = (jnp.einsum("bkginj,bknjd->bikgd", dscore, key_sel) * factor).astype(jnp.bfloat16)
        key_part = jnp.einsum("bkginj,bikgd->bknjd", dscore, query_tile) * factor
        value_part = jnp.einsum("bkginj,bikgd->bknjd", prob_low, grad_output)
        partial_value = partial_value.at[batch_index, chosen, :, kv_index, :].add(jnp.concatenate([key_part, value_part], axis=-1))
        return partial_value, (query_part, logit_grad)

    def source_step(total, source):
        tile_ids = source * tiles_dev + jnp.arange(tiles_dev, dtype=jnp.int32)
        fresh = jnp.zeros((BATCH, TILES, BLK, KVH, 2 * DH), jnp.float32)
        partial_value, parts = lax.scan(tile_step, fresh, tile_ids)
        rounded = lax.optimization_barrier(partial_value.astype(jnp.bfloat16)).astype(jnp.float32)
        return total + rounded, parts

    start_total = jnp.zeros((BATCH, TILES, BLK, KVH, 2 * DH), jnp.float32)
    summed_all, (query_parts, logit_parts) = lax.scan(source_step, start_total, jnp.arange(N_SEQ, dtype=jnp.int32))
    query_parts = query_parts.reshape((TILES,) + query_parts.shape[2:])
    logit_parts = logit_parts.reshape((TILES,) + logit_parts.shape[2:])
    query_grad = jnp.swapaxes(query_parts, 0, 1).reshape(BATCH, SEQLEN, HQ, DH)
    logit_rows = jnp.transpose(logit_parts.reshape(TILES, BATCH, BLK, HQ), (3, 1, 0, 2)).reshape(HQ, BATCH * SEQLEN)
    gate_weight_grad = jnp.dot(logit_rows, hidden.reshape(BATCH * SEQLEN, D), preferred_element_type=jnp.float32) * (1.0 / (BATCH * SEQLEN) ** 0.5)
    summed = summed_all.reshape(BATCH, SEQLEN, KVH, 2 * DH)
    return query_grad, summed[..., :DH].astype(jnp.bfloat16), summed[..., DH:].astype(jnp.bfloat16), gate_weight_grad
```

```python
import functools
import math

import jax
import jax.numpy as jnp
from jax import lax
from jax.experimental import pallas as pl
from jax.experimental.pallas import tpu as pltpu
from jax.sharding import PartitionSpec as P

LOG2E = math.log2(math.e)
F32 = jnp.float32
BF16 = jnp.bfloat16


def contract_last(a, b):
    return lax.dot_general(a, b, (((1,), (1,)), ((), ())), preferred_element_type=F32)


def matmul(a, b):
    return lax.dot_general(a, b, (((1,), (0,)), ((), ())), preferred_element_type=F32)


def halves(x):
    high = x.astype(BF16)
    return high, (x - high.astype(F32)).astype(BF16)


def rows_of(ref):
    x = ref[...]
    return x.astype(F32).reshape(x.shape[0] * x.shape[1], x.shape[2]).astype(BF16)


def spread_matrix(tokens, group):
    token = lax.broadcasted_iota(jnp.int32, (tokens, tokens * group), 0)
    column = lax.broadcasted_iota(jnp.int32, (tokens, tokens * group), 1)
    first = token * group
    return jnp.where((column >= first) & (column < first + group), 1.0, 0.0).astype(BF16)


def stats_kernel(upstream_ref, output_ref, gate_ref, total_ref, logit_ref, stat_ref):
    tokens, group, width = upstream_ref.shape
    rows = tokens * group
    spread = spread_matrix(tokens, group)
    product = (upstream_ref[...].astype(F32) * output_ref[...].astype(F32)).reshape(rows, width)
    high, low = halves(product)
    ones = jnp.ones((group, width), BF16)
    row_sum = contract_last(ones, high) + contract_last(ones, low)
    own = lax.broadcasted_iota(jnp.int32, (group, rows), 1) % group == lax.broadcasted_iota(
        jnp.int32, (group, rows), 0
    )
    picked_high, picked_low = halves(jnp.where(own, row_sum, 0.0))
    by_head = contract_last(picked_high, spread) + contract_last(picked_low, spread)
    gate = gate_ref[...]
    logit_ref[...] = (by_head * gate * (1.0 - gate)).astype(BF16)
    shift = (total_ref[...] - jnp.log(gate)) * LOG2E
    high, rest = shift.astype(BF16), shift - shift.astype(BF16).astype(F32)
    middle, low = halves(rest)
    wide = matmul(high, spread) + matmul(middle, spread) + matmul(low, spread)
    stat_ref[0:1, :] = jnp.sum(jnp.where(own, wide, 0.0), axis=0, keepdims=True)
    stat_ref[1:2, :] = row_sum[0:1, :]


def attend(key, key_turned, value, query, upstream, stats, factor, mask):
    scores = contract_last(key, query)
    prob = jnp.exp2(scores * (factor * LOG2E) - stats[0:1, :])
    if mask is not None:
        prob = jnp.where(mask, prob, 0.0)
    prob_grad = contract_last(value, upstream)
    dscore = (prob * (prob_grad - stats[1:2, :])).astype(BF16)
    key_part = matmul(dscore, query)
    value_part = matmul(prob.astype(BF16), upstream)
    query_turned = matmul(key_turned, dscore)
    return key_part, value_part, query_turned


def far_kernel(
    seq_ref, query_ref, upstream_ref, stat_ref, key_ref, value_ref, part_ref, turned_ref,
    q_rows, u_rows, *, factor, step
):
    rows = q_rows.shape[0]

    @pl.when(seq_ref[0] > 0)
    def _():
        q_rows[...] = rows_of(query_ref)
        u_rows[...] = rows_of(upstream_ref)
        key = key_ref[...]
        value = value_ref[...]
        key_turned = key.astype(F32).T.astype(BF16)
        key_sum = jnp.zeros(key.shape, F32)
        value_sum = jnp.zeros(key.shape, F32)
        for start in range(0, rows, step):
            at = slice(start, start + step)
            key_part, value_part, turned = attend(
                key, key_turned, value, q_rows[at, :], u_rows[at, :], stat_ref[:, at], factor, None
            )
            key_sum += key_part
            value_sum += value_part
            turned_ref[:, at] = (turned * factor).astype(BF16)
        part_ref[0] = (key_sum * factor).astype(BF16)
        part_ref[1] = value_sum.astype(BF16)

    @pl.when(seq_ref[0] == 0)
    def _():
        turned_ref[...] = jnp.zeros(turned_ref.shape, BF16)
        part_ref[...] = jnp.zeros(part_ref.shape, BF16)


def near_kernel(
    query_ref, upstream_ref, stat_ref, key_ref, value_ref, turned_ref, part_ref, grad_ref,
    q_rows, u_rows, key_sum, value_sum, *, factor, step
):
    rows = q_rows.shape[0]
    tokens, group, width = query_ref.shape
    q_rows[...] = rows_of(query_ref)
    u_rows[...] = rows_of(upstream_ref)
    key_turned = key_ref[...].astype(F32).T.astype(BF16)
    span = step // group
    for start in reversed(range(0, rows, step)):
        at = slice(start, start + step)
        first = start // group
        seen = first + span
        key_pos = lax.broadcasted_iota(jnp.int32, (seen, step), 0)
        column = lax.broadcasted_iota(jnp.int32, (seen, step), 1)
        mask = (key_pos - first) * group <= column
        key_part, value_part, turned = attend(
            key_ref[0:seen, :], key_turned[:, 0:seen], value_ref[0:seen, :],
            q_rows[at, :], u_rows[at, :], stat_ref[:, at], factor, mask
        )
        if seen == tokens:
            key_sum[...] = key_part
            value_sum[...] = value_part
        else:
            key_sum[0:seen, :] += key_part
            value_sum[0:seen, :] += value_part
        total = turned * factor + turned_ref[:, at].astype(F32)
        grad_ref[first:seen] = total.T.reshape(span, group, width).astype(BF16)
    part_ref[0] = (key_sum[...] * factor).astype(BF16)
    part_ref[1] = value_sum[...].astype(BF16)


def gate_kernel(place_ref, *refs, heads_count, members):
    logit_refs = refs[:heads_count]
    hidden_ref = refs[heads_count]
    out_refs = refs[heads_count + 1 : heads_count + 1 + members]
    every, product = refs[heads_count + 1 + members :]
    here = logit_refs[0].shape[0]
    for other in range(heads_count):
        at = pl.multiple_of((place_ref[0] ^ other) * here, here)
        every[pl.ds(at, here), :] = logit_refs[other][...].astype(F32)
    product[...] = matmul(every[...].astype(BF16), hidden_ref[...])
    rows = product.shape[0] // members
    for other in range(members):
        at = pl.multiple_of((place_ref[1] ^ other) * rows, rows)
        out_refs[other][...] = product[pl.ds(at, rows), :].astype(BF16)


def join_kernel(place_ref, *refs):
    out_ref = refs[-1]
    rows = refs[0].shape[0]
    for other, ref in enumerate(refs[:-1]):
        at = pl.multiple_of((place_ref[1] ^ other) * rows, rows)
        out_ref[pl.ds(at, rows), :] = ref[...].astype(F32)


def exchange(x, axes, size, other):
    return lax.ppermute(x, axes, [(i, i ^ other) for i in range(size)])


def dense_on_device(
    queries, keys, values, attn_out, out_grad, gate_values, log_totals, hidden,
    block_ids, block_valid
):
    tokens, heads, width = queries.shape[1:]
    kv_heads = keys.shape[2]
    group = heads // kv_heads
    rows = tokens * group
    step = tokens // block_ids.shape[1] * group
    factor = width ** (-0.5)
    head_count = lax.axis_size("head")
    seq_count = lax.axis_size("seq")
    members = seq_count * lax.axis_size("dp")
    seq_at = lax.axis_index("seq").astype(jnp.int32)[None]
    place = jnp.stack(
        [lax.axis_index("head"), lax.axis_index(("seq", "dp"))]
    ).astype(jnp.int32)

    key_own = jnp.transpose(keys[0], (1, 0, 2))
    value_own = jnp.transpose(values[0], (1, 0, 2))
    key_far = lax.ppermute(key_own, "seq", [(0, 1)])
    value_far = lax.ppermute(value_own, "seq", [(0, 1)])

    split = (tokens, kv_heads, group, width)
    query_view = queries.reshape(split)
    upstream_view = out_grad.reshape(split)
    output_view = attn_out.reshape(split)

    wide_spec = pl.BlockSpec((tokens, None, group, width), lambda k: (0, k, 0, 0))
    kv_spec = pl.BlockSpec((None, tokens, width), lambda k: (k, 0, 0))
    head_spec = pl.BlockSpec((None, group, tokens), lambda k: (k, 0, 0))
    stat_spec = pl.BlockSpec((None, 2, rows), lambda k: (k, 0, 0))
    part_spec = pl.BlockSpec((2, None, tokens, width), lambda k: (0, k, 0, 0))
    turned_spec = pl.BlockSpec((None, width, rows), lambda k: (k, 0, 0))
    smem = pl.BlockSpec(memory_space=pltpu.SMEM)
    params = pltpu.CompilerParams(vmem_limit_bytes=48 << 20)
    row_scratch = [pltpu.VMEM((rows, width), BF16)] * 2

    logit, stats = pl.pallas_call(
        stats_kernel,
        grid=(kv_heads,),
        in_specs=[wide_spec, wide_spec, head_spec, head_spec],
        out_specs=[head_spec, stat_spec],
        out_shape=[
            jax.ShapeDtypeStruct((kv_heads, group, tokens), BF16),
            jax.ShapeDtypeStruct((kv_heads, 2, rows), F32),
        ],
        compiler_params=params,
        name="stats",
    )(
        upstream_view,
        output_view,
        gate_values.reshape(kv_heads, group, tokens),
        log_totals.reshape(kv_heads, group, tokens),
    )
    logit = logit.reshape(heads, tokens)
    logits = [logit] + [exchange(logit, "head", head_count, o) for o in range(1, head_count)]

    chunk = head_count * heads // members
    model = hidden.shape[2]
    chunks = pl.pallas_call(
        functools.partial(gate_kernel, heads_count=head_count, members=members),
        in_specs=[smem] + [pl.BlockSpec(memory_space=pltpu.VMEM)] * (head_count + 1),
        out_specs=[pl.BlockSpec(memory_space=pltpu.VMEM)] * members,
        out_shape=[jax.ShapeDtypeStruct((chunk, model), BF16)] * members,
        scratch_shapes=[
            pltpu.VMEM((head_count * heads, tokens), F32),
            pltpu.VMEM((head_count * heads, model), F32),
        ],
        compiler_params=params,
        name="gate",
    )(place, *logits, hidden[0])
    *chunks, stats = lax.optimization_barrier((*chunks, stats))
    terms = [chunks[0]] + [
        exchange(chunks[o], ("seq", "dp"), members, o) for o in range(1, members)
    ]

    far_parts, turned = pl.pallas_call(
        functools.partial(far_kernel, factor=factor, step=step),
        grid=(kv_heads,),
        in_specs=[smem, wide_spec, wide_spec, stat_spec, kv_spec, kv_spec],
        out_specs=[part_spec, turned_spec],
        out_shape=[
            jax.ShapeDtypeStruct((2, kv_heads, tokens, width), BF16),
            jax.ShapeDtypeStruct((kv_heads, width, rows), BF16),
        ],
        scratch_shapes=row_scratch,
        compiler_params=params,
        name="far",
    )(seq_at, query_view, upstream_view, stats, key_far, value_far)
    terms = list(lax.optimization_barrier((*terms, turned)))
    turned = terms.pop()
    got_parts = lax.ppermute(far_parts, "seq", [(1, 0)])

    weight_scale = 1.0 / math.sqrt(members * tokens)
    reduced = (sum(t.astype(F32) for t in terms) * weight_scale).astype(BF16)
    reduced, turned = lax.optimization_barrier((reduced, turned))
    pieces = [reduced] + [
        exchange(reduced, ("seq", "dp"), members, o) for o in range(1, members)
    ]

    near_parts, query_grad = pl.pallas_call(
        functools.partial(near_kernel, factor=factor, step=step),
        grid=(kv_heads,),
        in_specs=[wide_spec, wide_spec, stat_spec, kv_spec, kv_spec, turned_spec],
        out_specs=[part_spec, wide_spec],
        out_shape=[
            jax.ShapeDtypeStruct((2, kv_heads, tokens, width), BF16),
            jax.ShapeDtypeStruct(split, BF16),
        ],
        scratch_shapes=row_scratch + [pltpu.VMEM((tokens, width), F32)] * 2,
        compiler_params=params,
        name="near",
    )(query_view, upstream_view, stats, key_own, value_own, turned)

    gate_weight_grad = pl.pallas_call(
        join_kernel,
        in_specs=[smem] + [pl.BlockSpec(memory_space=pltpu.VMEM)] * members,
        out_specs=pl.BlockSpec(memory_space=pltpu.VMEM),
        out_shape=jax.ShapeDtypeStruct((head_count * heads, model), F32),
        compiler_params=params,
        name="join",
    )(place, *pieces)
    summed = (near_parts.astype(F32) + got_parts.astype(F32)).astype(BF16)
    return (
        query_grad.reshape(1, tokens, heads, width),
        jnp.transpose(summed[0], (1, 0, 2))[None],
        jnp.transpose(summed[1], (1, 0, 2))[None],
        gate_weight_grad,
    )


def is_power(n):
    return n & (n - 1) == 0


def on_device(*args):
    queries, keys, block_ids = args[0], args[1], args[8]
    seq_count = lax.axis_size("seq")
    head_count = lax.axis_size("head")
    members = seq_count * lax.axis_size("dp")
    all_blocks = block_ids.shape[1] * seq_count
    if (
        all_blocks <= block_ids.shape[3]
        and seq_count == 2
        and is_power(members)
        and is_power(head_count)
        and head_count * queries.shape[2] % (8 * members) == 0
        and queries.shape[2] // keys.shape[2] == 8
    ):
        return dense_on_device(*args)
    return selected_on_device(*args)


def selected_on_device(
    queries,
    keys,
    values,
    attn_out,
    out_grad,
    gate_values,
    log_totals,
    hidden,
    block_ids,
    block_valid,
):
    tokens_here = queries.shape[1]
    heads_here = queries.shape[2]
    kv_heads = keys.shape[2]
    head_width = queries.shape[3]
    group_size = heads_here // kv_heads
    tiles_here = block_ids.shape[1]
    block_rows = tokens_here // tiles_here
    seq_count = lax.axis_size("seq")
    all_blocks = tiles_here * seq_count
    factor = head_width ** (-0.5)
    chosen = block_ids[0]
    usable = block_valid[0] > 0
    head_rows = jnp.arange(kv_heads, dtype=jnp.int32)[None, :, None]
    offsets = jnp.arange(block_rows, dtype=jnp.int32)
    whole_keys, whole_values = (
        lax.all_gather(keys, "seq", axis=1, tiled=True),
        lax.all_gather(values, "seq", axis=1, tiled=True),
    )
    key_sel = whole_keys[0].reshape(all_blocks, block_rows, kv_heads, head_width)[
        chosen, :, head_rows, :
    ]
    value_sel = whole_values[0].reshape(all_blocks, block_rows, kv_heads, head_width)[
        chosen, :, head_rows, :
    ]
    query_tiles = queries[0].reshape(tiles_here, block_rows, kv_heads, group_size, head_width)
    output_tiles = attn_out[0].reshape(tiles_here, block_rows, kv_heads, group_size, head_width)
    upstream_tiles = out_grad[0].reshape(tiles_here, block_rows, kv_heads, group_size, head_width)
    gate_tiles = jnp.transpose(
        gate_values[0].reshape(kv_heads, group_size, tiles_here, block_rows), (2, 0, 1, 3)
    )
    total_tiles = jnp.transpose(
        log_totals[0].reshape(kv_heads, group_size, tiles_here, block_rows), (2, 0, 1, 3)
    )
    tile_numbers = lax.axis_index("seq") * tiles_here + jnp.arange(tiles_here, dtype=jnp.int32)

    def tile_math(tile_items):
        (
            tile_number,
            query_tile,
            output_tile,
            upstream,
            gate_tile,
            totals,
            picked,
            usable_tile,
            key_tile,
            value_tile,
        ) = tile_items
        gates_by_row = jnp.transpose(gate_tile, (2, 0, 1))
        grad_output = (gates_by_row[..., None] * upstream.astype(jnp.float32)).astype(jnp.bfloat16)
        output_wide = output_tile.astype(jnp.float32)
        row_delta = jnp.transpose(
            jnp.sum(grad_output.astype(jnp.float32) * output_wide, axis=-1), (1, 2, 0)
        )
        gate_grad = jnp.sum(upstream.astype(jnp.float32) * output_wide, axis=-1)
        logit_grad = (gate_grad * gates_by_row * (1.0 - gates_by_row)).astype(jnp.bfloat16)
        scores = (
            jnp.einsum("ikgd,knjd->kginj", query_tile, key_tile, preferred_element_type=jnp.float32)
            * factor
        )
        query_pos = tile_number * block_rows + offsets
        key_pos = picked[..., None] * block_rows + offsets
        allowed = usable_tile[:, None, :, None] & (
            key_pos[:, None, :, :] <= query_pos[None, :, None, None]
        )
        probability = jnp.where(allowed[:, None], jnp.exp(scores - totals[..., None, None]), 0.0)
        prob_grad = jnp.einsum(
            "ikgd,knjd->kginj", grad_output, value_tile, preferred_element_type=jnp.float32
        )
        dscore = (probability * (prob_grad - row_delta[..., None, None])).astype(jnp.bfloat16)
        prob_low = probability.astype(jnp.bfloat16)
        query_part = (
            jnp.einsum("kginj,knjd->ikgd", dscore, key_tile, preferred_element_type=jnp.float32)
            * factor
        ).astype(jnp.bfloat16)
        key_part = (
            jnp.einsum("kginj,ikgd->knjd", dscore, query_tile, preferred_element_type=jnp.float32)
            * factor
        )
        value_part = jnp.einsum(
            "kginj,ikgd->knjd", prob_low, grad_output, preferred_element_type=jnp.float32
        )
        return (query_part, logit_grad, jnp.concatenate([key_part, value_part], axis=-1))

    def tile_step(partial_value, tile_items):
        query_part, logit_grad, paired = tile_math(tile_items)
        return (partial_value, (query_part, logit_grad, paired))

    tile_items = (
        tile_numbers,
        query_tiles,
        output_tiles,
        upstream_tiles,
        gate_tiles,
        total_tiles,
        chosen,
        usable,
        key_sel,
        value_sel,
    )
    unused, (query_parts, logit_parts, paired_all) = lax.scan(
        tile_step, jnp.zeros((), jnp.float32), tile_items
    )
    span_blocks = tokens_here * lax.axis_size("seq") // block_rows
    target = chosen
    target = jnp.where((target >= 0) & (target < span_blocks), target, span_blocks)
    holder = jnp.zeros((span_blocks, block_rows, kv_heads, 2 * head_width), jnp.float32)
    holder = holder.at[target, :, head_rows, :].add(paired_all, mode="drop")
    summed = lax.psum_scatter(
        holder.reshape(tokens_here * lax.axis_size("seq"), kv_heads, 2 * head_width).astype(
            jnp.bfloat16
        ),
        "seq",
        scatter_dimension=0,
        tiled=True,
    ).astype(jnp.float32)
    query_grad = query_parts.reshape(1, tokens_here, heads_here, head_width)
    logit_rows = jnp.transpose(logit_parts.reshape(tokens_here, heads_here))[None]
    every_logit = lax.all_gather(logit_rows, "head", axis=1, tiled=True)
    weight_part = jnp.dot(every_logit[0], hidden[0], preferred_element_type=jnp.float32)
    weight_scale = 1.0 / math.sqrt(lax.axis_size("dp") * seq_count * tokens_here)
    gate_weight_grad = lax.psum(weight_part, ("seq", "dp")) * weight_scale
    key_grad = summed[None, :, :, :head_width].astype(jnp.bfloat16)
    value_grad = summed[None, :, :, head_width:].astype(jnp.bfloat16)
    return (query_grad, key_grad, value_grad, gate_weight_grad)


def solution(mesh):
    return jax.shard_map(
        on_device,
        mesh=mesh,
        in_specs=(
            P("dp", "seq", "head", None),
            P("dp", "seq", "head", None),
            P("dp", "seq", "head", None),
            P("dp", "seq", "head", None),
            P("dp", "seq", "head", None),
            P("dp", "head", "seq"),
            P("dp", "head", "seq"),
            P("dp", "seq", "head"),
            P("dp", "seq", "head", None),
            P("dp", "seq", "head", None),
        ),
        out_specs=(
            P("dp", "seq", "head", None),
            P("dp", "seq", "head", None),
            P("dp", "seq", "head", None),
            P(None, "head"),
        ),
        check_vma=False,
    )
```

```python
import functools
import math

import jax
import jax.numpy as jnp
from jax import lax
from jax.experimental import pallas as pl
from jax.experimental.pallas import tpu as pltpu
from jax.sharding import PartitionSpec as P

LOG2E = math.log2(math.e)
F32 = jnp.float32
BF16 = jnp.bfloat16


def contract_last(a, b):
    return lax.dot_general(a, b, (((1,), (1,)), ((), ())), preferred_element_type=F32)


def matmul(a, b):
    return lax.dot_general(a, b, (((1,), (0,)), ((), ())), preferred_element_type=F32)


def rows_of(ref):
    x = ref[...]
    return x.astype(F32).reshape(x.shape[0] * x.shape[1], x.shape[2]).astype(BF16)


def spread_matrix(tokens, group):
    token = lax.broadcasted_iota(jnp.int32, (tokens, tokens * group), 0)
    column = lax.broadcasted_iota(jnp.int32, (tokens, tokens * group), 1)
    first = token * group
    return jnp.where((column >= first) & (column < first + group), 1.0, 0.0).astype(BF16)


def stats_kernel(upstream_ref, output_ref, gate_ref, total_ref, logit_ref, stat_ref, *, piece):
    tokens, group, width = upstream_ref.shape
    rows = piece * group
    spread = spread_matrix(piece, group)
    ones = jnp.ones((group, width), BF16)
    own = lax.broadcasted_iota(jnp.int32, (group, rows), 1) & (group - 1) == (
        lax.broadcasted_iota(jnp.int32, (group, rows), 0)
    )
    gate = gate_ref[...]
    slope = gate * (1.0 - gate)
    shift = (total_ref[...] - jnp.log(gate)) * LOG2E
    high = shift.astype(BF16).astype(F32)
    middle = (shift - high).astype(BF16).astype(F32)
    low = shift - high - middle
    shifts = jnp.concatenate([high, middle, low], axis=0).astype(BF16)
    for start in range(0, tokens, piece):
        some = slice(start, start + piece)
        at = slice(start * group, start * group + rows)
        product = upstream_ref[some].astype(F32) * output_ref[some].astype(F32)
        row_sum = contract_last(ones, product.reshape(rows, width).astype(BF16))
        picked = jnp.where(own, row_sum, 0.0)
        high = picked.astype(BF16).astype(F32)
        both = jnp.concatenate([high, picked - high], axis=0).astype(BF16)
        by_head = contract_last(both, spread)
        by_head = by_head[:group] + by_head[group:]
        logit_ref[:, some] = (by_head * slope[:, some]).astype(BF16)
        wide = matmul(shifts[:, some], spread)
        wide = wide[:group] + wide[group : 2 * group] + wide[2 * group :]
        stat_ref[0:1, at] = jnp.sum(jnp.where(own, wide, 0.0), axis=0, keepdims=True)
        stat_ref[1:2, at] = row_sum[0:1, :]


def pack_kernel(key_ref, value_ref, out_ref):
    for head in range(key_ref.shape[1]):
        out_ref[0, head] = key_ref[:, head, :]
        out_ref[1, head] = value_ref[:, head, :]


def add_kernel(a_ref, b_ref, out_ref):
    out_ref[...] = (a_ref[...].astype(F32) + b_ref[...].astype(F32)).astype(BF16)


def finish_kernel(near_refs, got_ref, a_ref, b_ref, key_ref, value_ref, out_ref, *, scale):
    out_ref[...] = (a_ref[...].astype(F32) + b_ref[...].astype(F32)) * scale
    for place, ref in enumerate((key_ref, value_ref)):
        ref[...] = jnp.stack(
            [
                near[place].astype(F32) + got_ref[place, head].astype(F32)
                for head, near in enumerate(near_refs)
            ],
            axis=1,
        ).astype(BF16)


def attend(key, key_turned, value, query, upstream, stats, factor, mask):
    scores = contract_last(key, query)
    prob = jnp.exp2(scores * (factor * LOG2E) - stats[0:1, :])
    if mask is not None:
        prob = jnp.where(mask, prob, 0.0)
    prob_grad = contract_last(value, upstream)
    dscore = (prob * (prob_grad - stats[1:2, :])).astype(BF16)
    key_part = matmul(dscore, query)
    value_part = matmul(prob.astype(BF16), upstream)
    query_turned = matmul(key_turned, dscore)
    return key_part, value_part, query_turned


def far_kernel(
    seq_ref, query_ref, upstream_ref, stat_ref, key_ref, value_ref, part_ref, turned_ref,
    q_rows, u_rows, *, factor, step
):
    rows = q_rows.shape[0]

    @pl.when(seq_ref[0] > 0)
    def _():
        q_rows[...] = rows_of(query_ref)
        u_rows[...] = rows_of(upstream_ref)
        key = key_ref[...]
        value = value_ref[...]
        key_turned = key.astype(F32).T.astype(BF16)
        key_sum = jnp.zeros(key.shape, F32)
        value_sum = jnp.zeros(key.shape, F32)
        for start in range(0, rows, step):
            at = slice(start, start + step)
            key_part, value_part, turned = attend(
                key, key_turned, value, q_rows[at, :], u_rows[at, :], stat_ref[:, at], factor, None
            )
            key_sum += key_part
            value_sum += value_part
            turned_ref[:, at] = (turned * factor).astype(BF16)
        part_ref[0] = (key_sum * factor).astype(BF16)
        part_ref[1] = value_sum.astype(BF16)

    @pl.when(seq_ref[0] == 0)
    def _():
        turned_ref[...] = jnp.zeros(turned_ref.shape, BF16)
        part_ref[...] = jnp.zeros(part_ref.shape, BF16)


def near_kernel(
    query_ref, upstream_ref, stat_ref, key_ref, value_ref, turned_ref, *refs, factor, step
):
    part_ref, grad_ref, q_rows, u_rows, key_sum, value_sum = refs[-6:]
    rows = q_rows.shape[0]
    tokens, group, width = query_ref.shape
    q_rows[...] = rows_of(query_ref)
    u_rows[...] = rows_of(upstream_ref)
    key_turned = key_ref[...].astype(F32).T.astype(BF16)
    span = step // group
    for start in reversed(range(0, rows, step)):
        at = slice(start, start + step)
        first = start // group
        seen = first + span
        key_pos = lax.broadcasted_iota(jnp.int32, (seen, step), 0)
        column = lax.broadcasted_iota(jnp.int32, (seen, step), 1)
        mask = (key_pos - first) * group <= column
        key_part, value_part, turned = attend(
            key_ref[0:seen, :], key_turned[:, 0:seen], value_ref[0:seen, :],
            q_rows[at, :], u_rows[at, :], stat_ref[:, at], factor, mask
        )
        if seen == tokens:
            key_sum[...] = key_part
            value_sum[...] = value_part
        else:
            key_sum[0:seen, :] += key_part
            value_sum[0:seen, :] += value_part
        total = turned * factor + turned_ref[:, at].astype(F32)
        grad_ref[first:seen] = total.T.reshape(span, group, width).astype(BF16)
    part_ref[0] = (key_sum[...] * factor).astype(BF16)
    part_ref[1] = value_sum[...].astype(BF16)


def gate_kernel(place_ref, *refs):
    *logit_refs, hidden_ref, out_ref, every = refs
    here = logit_refs[0].shape[0]
    for other, ref in enumerate(logit_refs):
        at = pl.multiple_of((place_ref[0] ^ other) * here, here)
        every[pl.ds(at, here), :] = ref[...].astype(F32)
    out_ref[...] = matmul(every[...].astype(BF16), hidden_ref[...]).astype(BF16)


def exchange(x, axes, size, other):
    return lax.ppermute(x, axes, [(i, i ^ other) for i in range(size)])


def dense_on_device(
    queries, keys, values, attn_out, out_grad, gate_values, log_totals, hidden,
    block_ids, block_valid
):
    tokens, heads, width = queries.shape[1:]
    kv_heads = keys.shape[2]
    group = heads // kv_heads
    rows = tokens * group
    step = tokens // block_ids.shape[1] * group
    factor = width ** (-0.5)
    head_count = lax.axis_size("head")
    dp_count = lax.axis_size("dp")
    members = lax.axis_size("seq") * dp_count
    seq_at = lax.axis_index("seq").astype(jnp.int32)[None]
    head_at = lax.axis_index("head").astype(jnp.int32)[None]
    whole = pl.BlockSpec(memory_space=pltpu.VMEM)
    smem = pl.BlockSpec(memory_space=pltpu.SMEM)
    params = pltpu.CompilerParams(vmem_limit_bytes=48 << 20)

    own = pl.pallas_call(
        pack_kernel,
        in_specs=[whole, whole],
        out_specs=whole,
        out_shape=jax.ShapeDtypeStruct((2, kv_heads, tokens, width), BF16),
        compiler_params=params,
        name="pack",
    )(keys[0], values[0])
    own, out_grad, attn_out = lax.optimization_barrier((own, out_grad, attn_out))
    far = lax.ppermute(own, "seq", [(0, 1)])

    split = (tokens, kv_heads, group, width)
    query_view = queries.reshape(split)
    upstream_view = out_grad.reshape(split)
    output_view = attn_out.reshape(split)

    def specs(at):
        wide = pl.BlockSpec((tokens, None, group, width), lambda k: (0, at(k), 0, 0))
        key = pl.BlockSpec((None, None, tokens, width), lambda k: (0, at(k), 0, 0))
        value = pl.BlockSpec((None, None, tokens, width), lambda k: (1, at(k), 0, 0))
        stat = pl.BlockSpec((None, 2, rows), lambda k: (at(k), 0, 0))
        turned = pl.BlockSpec((None, width, rows), lambda k: (at(k), 0, 0))
        return wide, key, value, stat, turned

    wide_spec, key_spec, value_spec, stat_spec, turned_spec = specs(lambda k: k)
    head_spec = pl.BlockSpec((None, group, tokens), lambda k: (k, 0, 0))
    part_spec = pl.BlockSpec((2, None, tokens, width), lambda k: (0, k, 0, 0))
    row_scratch = [pltpu.VMEM((rows, width), BF16)] * 2

    logit, stats = pl.pallas_call(
        functools.partial(stats_kernel, piece=math.gcd(tokens, 128)),
        grid=(kv_heads,),
        in_specs=[wide_spec, wide_spec, head_spec, head_spec],
        out_specs=[head_spec, stat_spec],
        out_shape=[
            jax.ShapeDtypeStruct((kv_heads, group, tokens), BF16),
            jax.ShapeDtypeStruct((kv_heads, 2, rows), F32),
        ],
        compiler_params=params,
        name="stats",
    )(
        upstream_view,
        output_view,
        gate_values.reshape(kv_heads, group, tokens),
        log_totals.reshape(kv_heads, group, tokens),
    )
    logit = logit.reshape(heads, tokens)
    logits = [logit] + [exchange(logit, "head", head_count, o) for o in range(1, head_count)]

    model = hidden.shape[2]
    weight_shape = (head_count * heads, model)
    weight = pl.pallas_call(
        gate_kernel,
        in_specs=[smem] + [whole] * (head_count + 1),
        out_specs=whole,
        out_shape=jax.ShapeDtypeStruct(weight_shape, BF16),
        scratch_shapes=[pltpu.VMEM((head_count * heads, tokens), F32)],
        compiler_params=params,
        name="gate",
    )(head_at, *logits, hidden[0])
    weight, stats = lax.optimization_barrier((weight, stats))

    def add(a, b):
        return pl.pallas_call(
            add_kernel,
            in_specs=[whole, whole],
            out_specs=whole,
            out_shape=jax.ShapeDtypeStruct(weight_shape, BF16),
            compiler_params=params,
            name="add",
        )(a, b)

    steps = [("seq", 2, 1)]
    reach = dp_count // 2
    while reach > 0:
        steps.append(("dp", dp_count, reach))
        reach //= 2
    other = exchange(weight, *steps[0])

    far_parts, turned = pl.pallas_call(
        functools.partial(far_kernel, factor=factor, step=step),
        grid=(kv_heads,),
        in_specs=[smem, wide_spec, wide_spec, stat_spec, key_spec, value_spec],
        out_specs=[part_spec, turned_spec],
        out_shape=[
            jax.ShapeDtypeStruct((2, kv_heads, tokens, width), BF16),
            jax.ShapeDtypeStruct((kv_heads, width, rows), BF16),
        ],
        scratch_shapes=row_scratch,
        compiler_params=params,
        name="far",
    )(seq_at, query_view, upstream_view, stats, far, far)
    got_parts = lax.ppermute(far_parts, "seq", [(1, 0)])

    near_parts = []
    query_grad = []
    for head in range(kv_heads):
        if head + 1 < len(steps):
            other, turned = lax.optimization_barrier((other, turned))
            weight = add(weight, other)
            weight, turned = lax.optimization_barrier((weight, turned))
            other = exchange(weight, *steps[head + 1])
        wide_one, key_one, value_one, stat_one, turned_one = specs(lambda k, head=head: head)
        near_part, *query_grad = pl.pallas_call(
            functools.partial(near_kernel, factor=factor, step=step),
            grid=(1,),
            in_specs=[wide_one, wide_one, stat_one, key_one, value_one, turned_one]
            + [pl.BlockSpec(memory_space=pl.ANY)] * len(query_grad),
            out_specs=[pl.BlockSpec((2, tokens, width), lambda k: (0, 0, 0)), wide_one],
            out_shape=[
                jax.ShapeDtypeStruct((2, tokens, width), BF16),
                jax.ShapeDtypeStruct(split, BF16),
            ],
            scratch_shapes=row_scratch + [pltpu.VMEM((tokens, width), F32)] * 2,
            input_output_aliases={6: 1} if query_grad else {},
            compiler_params=params,
            name="near",
        )(query_view, upstream_view, stats, own, own, turned, *query_grad)
        near_parts.append(near_part)
        near_part, turned = lax.optimization_barrier((near_part, turned))
    for after in steps[kv_heads + 1 :]:
        weight = add(weight, other)
        other = exchange(weight, *after)

    weight_scale = 1.0 / math.sqrt(members * tokens)
    key_grad, value_grad, gate_weight_grad = pl.pallas_call(
        lambda *refs: finish_kernel(refs[:kv_heads], *refs[kv_heads:], scale=weight_scale),
        in_specs=[whole] * (kv_heads + 3),
        out_specs=[whole] * 3,
        out_shape=[
            jax.ShapeDtypeStruct((tokens, kv_heads, width), BF16),
            jax.ShapeDtypeStruct((tokens, kv_heads, width), BF16),
            jax.ShapeDtypeStruct(weight_shape, F32),
        ],
        compiler_params=params,
        name="finish",
    )(*near_parts, got_parts, weight, other)
    return (
        query_grad[0].reshape(1, tokens, heads, width),
        key_grad[None],
        value_grad[None],
        gate_weight_grad,
    )


def is_power(n):
    return n & (n - 1) == 0


def on_device(*args):
    queries, keys, block_ids = args[0], args[1], args[8]
    seq_count = lax.axis_size("seq")
    head_count = lax.axis_size("head")
    members = seq_count * lax.axis_size("dp")
    all_blocks = block_ids.shape[1] * seq_count
    if (
        all_blocks <= block_ids.shape[3]
        and seq_count == 2
        and is_power(members)
        and is_power(head_count)
        and queries.shape[2] // keys.shape[2] == 8
    ):
        return dense_on_device(*args)
    return selected_on_device(*args)


def selected_on_device(
    queries,
    keys,
    values,
    attn_out,
    out_grad,
    gate_values,
    log_totals,
    hidden,
    block_ids,
    block_valid,
):
    tokens_here = queries.shape[1]
    heads_here = queries.shape[2]
    kv_heads = keys.shape[2]
    head_width = queries.shape[3]
    group_size = heads_here // kv_heads
    tiles_here = block_ids.shape[1]
    block_rows = tokens_here // tiles_here
    seq_count = lax.axis_size("seq")
    all_blocks = tiles_here * seq_count
    factor = head_width ** (-0.5)
    chosen = block_ids[0]
    usable = block_valid[0] > 0
    head_rows = jnp.arange(kv_heads, dtype=jnp.int32)[None, :, None]
    offsets = jnp.arange(block_rows, dtype=jnp.int32)
    whole_keys, whole_values = (
        lax.all_gather(keys, "seq", axis=1, tiled=True),
        lax.all_gather(values, "seq", axis=1, tiled=True),
    )
    key_sel = whole_keys[0].reshape(all_blocks, block_rows, kv_heads, head_width)[
        chosen, :, head_rows, :
    ]
    value_sel = whole_values[0].reshape(all_blocks, block_rows, kv_heads, head_width)[
        chosen, :, head_rows, :
    ]
    query_tiles = queries[0].reshape(tiles_here, block_rows, kv_heads, group_size, head_width)
    output_tiles = attn_out[0].reshape(tiles_here, block_rows, kv_heads, group_size, head_width)
    upstream_tiles = out_grad[0].reshape(tiles_here, block_rows, kv_heads, group_size, head_width)
    gate_tiles = jnp.transpose(
        gate_values[0].reshape(kv_heads, group_size, tiles_here, block_rows), (2, 0, 1, 3)
    )
    total_tiles = jnp.transpose(
        log_totals[0].reshape(kv_heads, group_size, tiles_here, block_rows), (2, 0, 1, 3)
    )
    tile_numbers = lax.axis_index("seq") * tiles_here + jnp.arange(tiles_here, dtype=jnp.int32)

    def tile_math(tile_items):
        (
            tile_number,
            query_tile,
            output_tile,
            upstream,
            gate_tile,
            totals,
            picked,
            usable_tile,
            key_tile,
            value_tile,
        ) = tile_items
        gates_by_row = jnp.transpose(gate_tile, (2, 0, 1))
        grad_output = (gates_by_row[..., None] * upstream.astype(jnp.float32)).astype(jnp.bfloat16)
        output_wide = output_tile.astype(jnp.float32)
        row_delta = jnp.transpose(
            jnp.sum(grad_output.astype(jnp.float32) * output_wide, axis=-1), (1, 2, 0)
        )
        gate_grad = jnp.sum(upstream.astype(jnp.float32) * output_wide, axis=-1)
        logit_grad = (gate_grad * gates_by_row * (1.0 - gates_by_row)).astype(jnp.bfloat16)
        scores = (
            jnp.einsum("ikgd,knjd->kginj", query_tile, key_tile, preferred_element_type=jnp.float32)
            * factor
        )
        query_pos = tile_number * block_rows + offsets
        key_pos = picked[..., None] * block_rows + offsets
        allowed = usable_tile[:, None, :, None] & (
            key_pos[:, None, :, :] <= query_pos[None, :, None, None]
        )
        probability = jnp.where(allowed[:, None], jnp.exp(scores - totals[..., None, None]), 0.0)
        prob_grad = jnp.einsum(
            "ikgd,knjd->kginj", grad_output, value_tile, preferred_element_type=jnp.float32
        )
        dscore = (probability * (prob_grad - row_delta[..., None, None])).astype(jnp.bfloat16)
        prob_low = probability.astype(jnp.bfloat16)
        query_part = (
            jnp.einsum("kginj,knjd->ikgd", dscore, key_tile, preferred_element_type=jnp.float32)
            * factor
        ).astype(jnp.bfloat16)
        key_part = (
            jnp.einsum("kginj,ikgd->knjd", dscore, query_tile, preferred_element_type=jnp.float32)
            * factor
        )
        value_part = jnp.einsum(
            "kginj,ikgd->knjd", prob_low, grad_output, preferred_element_type=jnp.float32
        )
        return (query_part, logit_grad, jnp.concatenate([key_part, value_part], axis=-1))

    def tile_step(partial_value, tile_items):
        query_part, logit_grad, paired = tile_math(tile_items)
        return (partial_value, (query_part, logit_grad, paired))

    tile_items = (
        tile_numbers,
        query_tiles,
        output_tiles,
        upstream_tiles,
        gate_tiles,
        total_tiles,
        chosen,
        usable,
        key_sel,
        value_sel,
    )
    unused, (query_parts, logit_parts, paired_all) = lax.scan(
        tile_step, jnp.zeros((), jnp.float32), tile_items
    )
    span_blocks = tokens_here * lax.axis_size("seq") // block_rows
    target = chosen
    target = jnp.where((target >= 0) & (target < span_blocks), target, span_blocks)
    holder = jnp.zeros((span_blocks, block_rows, kv_heads, 2 * head_width), jnp.float32)
    holder = holder.at[target, :, head_rows, :].add(paired_all, mode="drop")
    summed = lax.psum_scatter(
        holder.reshape(tokens_here * lax.axis_size("seq"), kv_heads, 2 * head_width).astype(
            jnp.bfloat16
        ),
        "seq",
        scatter_dimension=0,
        tiled=True,
    ).astype(jnp.float32)
    query_grad = query_parts.reshape(1, tokens_here, heads_here, head_width)
    logit_rows = jnp.transpose(logit_parts.reshape(tokens_here, heads_here))[None]
    every_logit = lax.all_gather(logit_rows, "head", axis=1, tiled=True)
    weight_part = jnp.dot(every_logit[0], hidden[0], preferred_element_type=jnp.float32)
    weight_scale = 1.0 / math.sqrt(lax.axis_size("dp") * seq_count * tokens_here)
    gate_weight_grad = lax.psum(weight_part, ("seq", "dp")) * weight_scale
    key_grad = summed[None, :, :, :head_width].astype(jnp.bfloat16)
    value_grad = summed[None, :, :, head_width:].astype(jnp.bfloat16)
    return (query_grad, key_grad, value_grad, gate_weight_grad)


def solution(mesh):
    return jax.shard_map(
        on_device,
        mesh=mesh,
        in_specs=(
            P("dp", "seq", "head", None),
            P("dp", "seq", "head", None),
            P("dp", "seq", "head", None),
            P("dp", "seq", "head", None),
            P("dp", "seq", "head", None),
            P("dp", "head", "seq"),
            P("dp", "head", "seq"),
            P("dp", "seq", "head"),
            P("dp", "seq", "head", None),
            P("dp", "seq", "head", None),
        ),
        out_specs=(
            P("dp", "seq", "head", None),
            P("dp", "seq", "head", None),
            P("dp", "seq", "head", None),
            P(None, "head"),
        ),
        check_vma=False,
    )
```

```python
import functools
import math

import jax
import jax.numpy as jnp
from jax import lax
from jax.experimental import pallas as pl
from jax.experimental.pallas import tpu as pltpu
from jax.sharding import PartitionSpec as P

LOG2E = math.log2(math.e)
F32 = jnp.float32
BF16 = jnp.bfloat16


def contract_last(a, b):
    return lax.dot_general(a, b, (((1,), (1,)), ((), ())), preferred_element_type=F32)


def matmul(a, b):
    return lax.dot_general(a, b, (((1,), (0,)), ((), ())), preferred_element_type=F32)


def rows_of(x):
    return x.astype(F32).reshape(x.shape[0] * x.shape[1], x.shape[2]).astype(BF16)


def spread_matrix(tokens, group):
    token = lax.broadcasted_iota(jnp.int32, (tokens, tokens * group), 0)
    column = lax.broadcasted_iota(jnp.int32, (tokens, tokens * group), 1)
    first = token * group
    return jnp.where((column >= first) & (column < first + group), 1.0, 0.0).astype(BF16)


def stats_kernel(
    upstream_hbm, output_hbm, key_hbm, value_hbm, gate_hbm, total_hbm,
    logit_ref, stat_ref, rows_ref, pack_ref,
    upstream_ref, output_ref, key_ref, value_ref, gate_ref, total_ref, sems, *, piece
):
    tokens, kv_heads, group, width = upstream_ref.shape
    loads = [(gate_hbm, gate_ref), (total_hbm, total_ref)]
    for start in range(0, tokens, piece):
        some = pl.ds(start, piece)
        for source, target in ((upstream_hbm, upstream_ref), (output_hbm, output_ref)):
            loads.append((source.at[some], target.at[some]))
    loads += [(key_hbm, key_ref), (value_hbm, value_ref)]
    loads = [pltpu.make_async_copy(*pair, sems.at[i]) for i, pair in enumerate(loads)]
    for load in loads:
        load.start()
    rows = piece * group
    spread = spread_matrix(piece, group)
    ones = jnp.ones((group, width), BF16)
    own = lax.broadcasted_iota(jnp.int32, (group, rows), 1) & (group - 1) == (
        lax.broadcasted_iota(jnp.int32, (group, rows), 0)
    )
    loads[0].wait()
    loads[1].wait()
    gate = gate_ref[...]
    slope = gate * (1.0 - gate)
    shift = (total_ref[...] - jnp.log(gate)) * LOG2E
    high = shift.astype(BF16).astype(F32)
    middle = (shift - high).astype(BF16).astype(F32)
    low = shift - high - middle
    for number, start in enumerate(range(0, tokens, piece)):
        loads[2 * number + 2].wait()
        loads[2 * number + 3].wait()
        some = slice(start, start + piece)
        at = slice(start * group, start * group + rows)
        for k in range(kv_heads):
            heads = slice(k * group, (k + 1) * group)
            upstream = upstream_ref[some, k].astype(F32).reshape(rows, width)
            rows_ref[k, at, :] = upstream.astype(BF16)
            product = upstream * output_ref[some, k].astype(F32).reshape(rows, width)
            row_sum = contract_last(ones, product.astype(BF16))
            picked = jnp.where(own, row_sum, 0.0)
            rounded = picked.astype(BF16).astype(F32)
            both = jnp.concatenate([rounded, picked - rounded], axis=0).astype(BF16)
            by_head = contract_last(both, spread)
            by_head = by_head[:group] + by_head[group:]
            logit_ref[heads, some] = (by_head * slope[heads, some]).astype(BF16)
            shifts = jnp.concatenate(
                [high[heads, some], middle[heads, some], low[heads, some]], axis=0
            ).astype(BF16)
            wide = matmul(shifts, spread)
            wide = wide[:group] + wide[group : 2 * group] + wide[2 * group :]
            stat_ref[k, 0:1, at] = jnp.sum(jnp.where(own, wide, 0.0), axis=0, keepdims=True)
            stat_ref[k, 1:2, at] = row_sum[0:1, :]
    loads[-2].wait()
    loads[-1].wait()
    for k in range(kv_heads):
        pack_ref[0, k] = key_ref[:, k, :]
        pack_ref[1, k] = value_ref[:, k, :]


def add_kernel(a_ref, b_ref, out_ref):
    out_ref[...] = (a_ref[...].astype(F32) + b_ref[...].astype(F32)).astype(BF16)


def finish_kernel(near_refs, got_ref, a_ref, b_ref, key_ref, value_ref, out_ref, *, scale):
    out_ref[...] = (a_ref[...].astype(F32) + b_ref[...].astype(F32)) * scale
    for place, ref in enumerate((key_ref, value_ref)):
        ref[...] = jnp.stack(
            [
                near[place].astype(F32) + got_ref[place, head].astype(F32)
                for head, near in enumerate(near_refs)
            ],
            axis=1,
        ).astype(BF16)


def attend(key, key_turned, value, query, upstream, stats, factor, mask):
    scores = contract_last(key, query)
    prob = jnp.exp2(scores * (factor * LOG2E) - stats[0:1, :])
    if mask is not None:
        prob = jnp.where(mask, prob, 0.0)
    prob_grad = contract_last(value, upstream)
    dscore = (prob * (prob_grad - stats[1:2, :])).astype(BF16)
    key_part = matmul(dscore, query)
    value_part = matmul(prob.astype(BF16), upstream)
    query_turned = matmul(key_turned, dscore)
    return key_part, value_part, query_turned


def far_kernel(
    seq_ref, query_ref, upstream_ref, stat_ref, pair_ref, first_ref,
    part_ref, turned_ref, grad_ref, *, factor, step
):
    kv_heads, rows = upstream_ref.shape[:2]
    group, width = query_ref.shape[2:]
    span = step // group

    @pl.when(seq_ref[0] > 0)
    def _():
        for k in range(kv_heads):
            query = rows_of(query_ref[:, k])
            key = pair_ref[0, k]
            value = pair_ref[1, k]
            key_turned = key.astype(F32).T.astype(BF16)
            key_sum = jnp.zeros(key.shape, F32)
            value_sum = jnp.zeros(key.shape, F32)
            for start in range(0, rows, step):
                at = slice(start, start + step)
                first = start // group
                key_part, value_part, turned = attend(
                    key, key_turned, value, query[at], upstream_ref[k, at, :],
                    stat_ref[k, :, at], factor, None
                )
                key_sum += key_part
                value_sum += value_part
                if k == 0:
                    total = turned * factor + first_ref[:, at].astype(F32)
                    grad_ref[first : first + span] = (
                        total.T.reshape(span, group, width).astype(BF16)
                    )
                else:
                    turned_ref[:, at] = (turned * factor).astype(BF16)
            part_ref[0, k] = (key_sum * factor).astype(BF16)
            part_ref[1, k] = value_sum.astype(BF16)

    @pl.when(seq_ref[0] == 0)
    def _():
        turned_ref[...] = jnp.zeros(turned_ref.shape, BF16)
        part_ref[...] = jnp.zeros(part_ref.shape, BF16)
        for start in range(0, rows, step):
            first = start // group
            total = first_ref[:, start : start + step].astype(F32)
            grad_ref[first : first + span] = total.T.reshape(span, group, width).astype(BF16)


def near_kernel(query_ref, upstream_ref, stat_ref, pair_ref, *refs, factor, step, k, last):
    key_sum, value_sum = refs[-2:]
    part_ref, grad_ref = refs[-4:-2]
    tokens, _, group, width = query_ref.shape
    rows = tokens * group
    query = rows_of(query_ref[:, k])
    key_turned = pair_ref[0, k].astype(F32).T.astype(BF16)
    span = step // group
    for start in reversed(range(0, rows, step)):
        at = slice(start, start + step)
        first = start // group
        seen = first + span
        key_pos = lax.broadcasted_iota(jnp.int32, (seen, step), 0)
        column = lax.broadcasted_iota(jnp.int32, (seen, step), 1)
        mask = (key_pos - first) * group <= column
        key_part, value_part, turned = attend(
            pair_ref[0, k, 0:seen, :], key_turned[:, 0:seen], pair_ref[1, k, 0:seen, :],
            query[at], upstream_ref[k, at, :], stat_ref[k, :, at], factor, mask
        )
        if seen == tokens:
            key_sum[...] = key_part
            value_sum[...] = value_part
        else:
            key_sum[0:seen, :] += key_part
            value_sum[0:seen, :] += value_part
        if last:
            total = turned * factor + refs[0][:, at].astype(F32)
            grad_ref[first:seen] = total.T.reshape(span, group, width).astype(BF16)
        else:
            grad_ref[:, at] = (turned * factor).astype(BF16)
    part_ref[0] = (key_sum[...] * factor).astype(BF16)
    part_ref[1] = value_sum[...].astype(BF16)


def gate_kernel(place_ref, *refs):
    *logit_refs, hidden_ref, out_ref, every = refs
    here = logit_refs[0].shape[0]
    for other, ref in enumerate(logit_refs):
        at = pl.multiple_of((place_ref[0] ^ other) * here, here)
        every[pl.ds(at, here), :] = ref[...].astype(F32)
    out_ref[...] = matmul(every[...].astype(BF16), hidden_ref[...]).astype(BF16)


def in_hbm(x):
    return pltpu.with_memory_space_constraint(x, pltpu.HBM)


def exchange(x, axes, size, other):
    return lax.ppermute(x, axes, [(i, i ^ other) for i in range(size)])


def dense_on_device(
    queries, keys, values, attn_out, out_grad, gate_values, log_totals, hidden,
    block_ids, block_valid
):
    tokens, heads, width = queries.shape[1:]
    kv_heads = keys.shape[2]
    group = heads // kv_heads
    rows = tokens * group
    step = tokens // block_ids.shape[1] * group
    factor = width ** (-0.5)
    head_count = lax.axis_size("head")
    dp_count = lax.axis_size("dp")
    members = lax.axis_size("seq") * dp_count
    seq_at = lax.axis_index("seq").astype(jnp.int32)[None]
    head_at = lax.axis_index("head").astype(jnp.int32)[None]
    whole = pl.BlockSpec(memory_space=pltpu.VMEM)
    smem = pl.BlockSpec(memory_space=pltpu.SMEM)
    params = pltpu.CompilerParams(vmem_limit_bytes=20 << 20)

    split = (tokens, kv_heads, group, width)
    query_view = queries.reshape(split)
    hbm = pl.BlockSpec(memory_space=pltpu.HBM)
    piece = math.gcd(tokens, 128)
    logit, stats, upstream, own = pl.pallas_call(
        functools.partial(stats_kernel, piece=piece),
        in_specs=[hbm] * 6,
        out_specs=[whole] * 4,
        out_shape=[
            jax.ShapeDtypeStruct((heads, tokens), BF16),
            jax.ShapeDtypeStruct((kv_heads, 2, rows), F32),
            jax.ShapeDtypeStruct((kv_heads, rows, width), BF16),
            jax.ShapeDtypeStruct((2, kv_heads, tokens, width), BF16),
        ],
        scratch_shapes=[
            pltpu.VMEM(split, BF16),
            pltpu.VMEM(split, BF16),
            pltpu.VMEM((tokens, kv_heads, width), BF16),
            pltpu.VMEM((tokens, kv_heads, width), BF16),
            pltpu.VMEM((heads, tokens), F32),
            pltpu.VMEM((heads, tokens), F32),
            pltpu.SemaphoreType.DMA((2 * (tokens // piece) + 4,)),
        ],
        compiler_params=params,
        name="stats",
    )(
        in_hbm(out_grad.reshape(split)), in_hbm(attn_out.reshape(split)),
        in_hbm(keys[0]), in_hbm(values[0]), in_hbm(gate_values[0]), in_hbm(log_totals[0]),
    )
    logits = [logit] + [exchange(logit, "head", head_count, o) for o in range(1, head_count)]
    far = lax.ppermute(own, "seq", [(0, 1)])

    grad_spec = [
        pl.BlockSpec((tokens, None, group, width), lambda k, head=head: (0, head, 0, 0))
        for head in range(kv_heads)
    ]
    grad_shape = jax.ShapeDtypeStruct(split, BF16)
    turned_shape = jax.ShapeDtypeStruct((width, rows), BF16)
    near_shape = jax.ShapeDtypeStruct((2, tokens, width), BF16)
    sums = [pltpu.VMEM((tokens, width), F32)] * 2
    near_first, turned_first = pl.pallas_call(
        functools.partial(near_kernel, factor=factor, step=step, k=0, last=False),
        in_specs=[whole] * 4,
        out_specs=[whole] * 2,
        out_shape=[near_shape, turned_shape],
        scratch_shapes=sums,
        compiler_params=params,
        name="near_first",
    )(query_view, upstream, stats, own)
    *logits, turned_first = lax.optimization_barrier((*logits, turned_first))

    model = hidden.shape[2]
    weight_shape = (head_count * heads, model)
    weight = pl.pallas_call(
        gate_kernel,
        in_specs=[smem] + [whole] * (head_count + 1),
        out_specs=whole,
        out_shape=jax.ShapeDtypeStruct(weight_shape, BF16),
        scratch_shapes=[pltpu.VMEM((head_count * heads, tokens), F32)],
        compiler_params=params,
        name="gate",
    )(head_at, *logits, hidden[0])
    weight, turned_first = lax.optimization_barrier((weight, turned_first))

    def add(a, b):
        return pl.pallas_call(
            add_kernel,
            in_specs=[whole, whole],
            out_specs=whole,
            out_shape=jax.ShapeDtypeStruct(weight_shape, BF16),
            compiler_params=params,
            name="add",
        )(a, b)

    steps = [("seq", 2, 1)]
    reach = dp_count // 2
    while reach > 0:
        steps.append(("dp", dp_count, reach))
        reach //= 2
    other = exchange(weight, *steps[0])

    far_parts, turned, query_grad = pl.pallas_call(
        functools.partial(far_kernel, factor=factor, step=step),
        grid=(1,),
        in_specs=[smem] + [whole] * 5,
        out_specs=[whole, whole, grad_spec[0]],
        out_shape=[
            jax.ShapeDtypeStruct((2, kv_heads, tokens, width), BF16), turned_shape, grad_shape
        ],
        compiler_params=params,
        name="far",
    )(seq_at, query_view, upstream, stats, far, turned_first)
    got_parts = lax.ppermute(far_parts, "seq", [(1, 0)])

    for after in steps[1:]:
        other, turned = lax.optimization_barrier((other, turned))
        weight = add(weight, other)
        if after is steps[1]:
            weight, turned = lax.optimization_barrier((weight, turned))
        other = exchange(weight, *after)
        if after is steps[1]:
            near_last, query_grad = pl.pallas_call(
                functools.partial(near_kernel, factor=factor, step=step, k=1, last=True),
                grid=(1,),
                in_specs=[whole] * 5 + [pl.BlockSpec(memory_space=pl.ANY)],
                out_specs=[whole, grad_spec[1]],
                out_shape=[near_shape, grad_shape],
                scratch_shapes=sums,
                input_output_aliases={5: 1},
                compiler_params=params,
                name="near_last",
            )(query_view, upstream, stats, own, turned, query_grad)
            near_last, turned = lax.optimization_barrier((near_last, turned))

    weight_scale = 1.0 / math.sqrt(members * tokens)
    key_grad, value_grad, gate_weight_grad = pl.pallas_call(
        lambda *refs: finish_kernel(refs[:kv_heads], *refs[kv_heads:], scale=weight_scale),
        in_specs=[whole] * (kv_heads + 3),
        out_specs=[whole] * 3,
        out_shape=[
            jax.ShapeDtypeStruct((tokens, kv_heads, width), BF16),
            jax.ShapeDtypeStruct((tokens, kv_heads, width), BF16),
            jax.ShapeDtypeStruct(weight_shape, F32),
        ],
        compiler_params=params,
        name="finish",
    )(near_first, near_last, got_parts, weight, other)
    return (
        query_grad.reshape(1, tokens, heads, width),
        key_grad[None],
        value_grad[None],
        gate_weight_grad,
    )


def is_power(n):
    return n & (n - 1) == 0


def on_device(*args):
    queries, keys, block_ids = args[0], args[1], args[8]
    seq_count = lax.axis_size("seq")
    head_count = lax.axis_size("head")
    members = seq_count * lax.axis_size("dp")
    all_blocks = block_ids.shape[1] * seq_count
    if (
        all_blocks <= block_ids.shape[3]
        and seq_count == 2
        and keys.shape[2] == 2
        and members > 2
        and is_power(members)
        and is_power(head_count)
        and queries.shape[2] // keys.shape[2] == 8
    ):
        return dense_on_device(*args)
    return selected_on_device(*args)


def selected_on_device(
    queries,
    keys,
    values,
    attn_out,
    out_grad,
    gate_values,
    log_totals,
    hidden,
    block_ids,
    block_valid,
):
    tokens_here = queries.shape[1]
    heads_here = queries.shape[2]
    kv_heads = keys.shape[2]
    head_width = queries.shape[3]
    group_size = heads_here // kv_heads
    tiles_here = block_ids.shape[1]
    block_rows = tokens_here // tiles_here
    seq_count = lax.axis_size("seq")
    all_blocks = tiles_here * seq_count
    factor = head_width ** (-0.5)
    chosen = block_ids[0]
    usable = block_valid[0] > 0
    head_rows = jnp.arange(kv_heads, dtype=jnp.int32)[None, :, None]
    offsets = jnp.arange(block_rows, dtype=jnp.int32)
    whole_keys, whole_values = (
        lax.all_gather(keys, "seq", axis=1, tiled=True),
        lax.all_gather(values, "seq", axis=1, tiled=True),
    )
    key_sel = whole_keys[0].reshape(all_blocks, block_rows, kv_heads, head_width)[
        chosen, :, head_rows, :
    ]
    value_sel = whole_values[0].reshape(all_blocks, block_rows, kv_heads, head_width)[
        chosen, :, head_rows, :
    ]
    query_tiles = queries[0].reshape(tiles_here, block_rows, kv_heads, group_size, head_width)
    output_tiles = attn_out[0].reshape(tiles_here, block_rows, kv_heads, group_size, head_width)
    upstream_tiles = out_grad[0].reshape(tiles_here, block_rows, kv_heads, group_size, head_width)
    gate_tiles = jnp.transpose(
        gate_values[0].reshape(kv_heads, group_size, tiles_here, block_rows), (2, 0, 1, 3)
    )
    total_tiles = jnp.transpose(
        log_totals[0].reshape(kv_heads, group_size, tiles_here, block_rows), (2, 0, 1, 3)
    )
    tile_numbers = lax.axis_index("seq") * tiles_here + jnp.arange(tiles_here, dtype=jnp.int32)

    def tile_math(tile_items):
        (
            tile_number,
            query_tile,
            output_tile,
            upstream,
            gate_tile,
            totals,
            picked,
            usable_tile,
            key_tile,
            value_tile,
        ) = tile_items
        gates_by_row = jnp.transpose(gate_tile, (2, 0, 1))
        grad_output = (gates_by_row[..., None] * upstream.astype(jnp.float32)).astype(jnp.bfloat16)
        output_wide = output_tile.astype(jnp.float32)
        row_delta = jnp.transpose(
            jnp.sum(grad_output.astype(jnp.float32) * output_wide, axis=-1), (1, 2, 0)
        )
        gate_grad = jnp.sum(upstream.astype(jnp.float32) * output_wide, axis=-1)
        logit_grad = (gate_grad * gates_by_row * (1.0 - gates_by_row)).astype(jnp.bfloat16)
        scores = (
            jnp.einsum("ikgd,knjd->kginj", query_tile, key_tile, preferred_element_type=jnp.float32)
            * factor
        )
        query_pos = tile_number * block_rows + offsets
        key_pos = picked[..., None] * block_rows + offsets
        allowed = usable_tile[:, None, :, None] & (
            key_pos[:, None, :, :] <= query_pos[None, :, None, None]
        )
        probability = jnp.where(allowed[:, None], jnp.exp(scores - totals[..., None, None]), 0.0)
        prob_grad = jnp.einsum(
            "ikgd,knjd->kginj", grad_output, value_tile, preferred_element_type=jnp.float32
        )
        dscore = (probability * (prob_grad - row_delta[..., None, None])).astype(jnp.bfloat16)
        prob_low = probability.astype(jnp.bfloat16)
        query_part = (
            jnp.einsum("kginj,knjd->ikgd", dscore, key_tile, preferred_element_type=jnp.float32)
            * factor
        ).astype(jnp.bfloat16)
        key_part = (
            jnp.einsum("kginj,ikgd->knjd", dscore, query_tile, preferred_element_type=jnp.float32)
            * factor
        )
        value_part = jnp.einsum(
            "kginj,ikgd->knjd", prob_low, grad_output, preferred_element_type=jnp.float32
        )
        return (query_part, logit_grad, jnp.concatenate([key_part, value_part], axis=-1))

    def tile_step(partial_value, tile_items):
        query_part, logit_grad, paired = tile_math(tile_items)
        return (partial_value, (query_part, logit_grad, paired))

    tile_items = (
        tile_numbers,
        query_tiles,
        output_tiles,
        upstream_tiles,
        gate_tiles,
        total_tiles,
        chosen,
        usable,
        key_sel,
        value_sel,
    )
    unused, (query_parts, logit_parts, paired_all) = lax.scan(
        tile_step, jnp.zeros((), jnp.float32), tile_items
    )
    span_blocks = tokens_here * lax.axis_size("seq") // block_rows
    target = chosen
    target = jnp.where((target >= 0) & (target < span_blocks), target, span_blocks)
    holder = jnp.zeros((span_blocks, block_rows, kv_heads, 2 * head_width), jnp.float32)
    holder = holder.at[target, :, head_rows, :].add(paired_all, mode="drop")
    summed = lax.psum_scatter(
        holder.reshape(tokens_here * lax.axis_size("seq"), kv_heads, 2 * head_width).astype(
            jnp.bfloat16
        ),
        "seq",
        scatter_dimension=0,
        tiled=True,
    ).astype(jnp.float32)
    query_grad = query_parts.reshape(1, tokens_here, heads_here, head_width)
    logit_rows = jnp.transpose(logit_parts.reshape(tokens_here, heads_here))[None]
    every_logit = lax.all_gather(logit_rows, "head", axis=1, tiled=True)
    weight_part = jnp.dot(every_logit[0], hidden[0], preferred_element_type=jnp.float32)
    weight_scale = 1.0 / math.sqrt(lax.axis_size("dp") * seq_count * tokens_here)
    gate_weight_grad = lax.psum(weight_part, ("seq", "dp")) * weight_scale
    key_grad = summed[None, :, :, :head_width].astype(jnp.bfloat16)
    value_grad = summed[None, :, :, head_width:].astype(jnp.bfloat16)
    return (query_grad, key_grad, value_grad, gate_weight_grad)


def solution(mesh):
    return jax.shard_map(
        on_device,
        mesh=mesh,
        in_specs=(
            P("dp", "seq", "head", None),
            P("dp", "seq", "head", None),
            P("dp", "seq", "head", None),
            P("dp", "seq", "head", None),
            P("dp", "seq", "head", None),
            P("dp", "head", "seq"),
            P("dp", "head", "seq"),
            P("dp", "seq", "head"),
            P("dp", "seq", "head", None),
            P("dp", "seq", "head", None),
        ),
        out_specs=(
            P("dp", "seq", "head", None),
            P("dp", "seq", "head", None),
            P("dp", "seq", "head", None),
            P(None, "head"),
        ),
        check_vma=False,
    )
```
